32 devices in a mesh: row: 8 (over y, x, core), col: 4 (over z).
Axes of the slice: x: 2, y: 2, z: 4, core: 2. Of those that a mesh axis runs over, the one named last changes fastest.
Arguments:
- earlier_blocks: bfloat16 [32, 8, 128, 128], P('row', 'col'), may hold values from -0.5 to 0.5
- later_blocks: bfloat16 [8, 32, 128, 128], P('row', 'col'), may hold values from -6 to 6
- earlier_pattern: int32 [32, 8], P('row', 'col'), may hold values from 0 to 1, as said below
- later_pattern: int32 [8, 32], P('row', 'col'), may hold values from 0 to 1, as said below
- triples: int32 [32, 32, 48], P('row', 'col'), may hold values from 0 to 7
Outputs:
- composed: float32 [32, 32, 128, 128], P('row', 'col')
The draws below stay inside these ranges and needn't reach their ends.
Inputs may be any that keep to these rules, and one draw needn't show every extreme that they name: `earlier_pattern`: in each aligned share of 4 x 2 entries held by one device, at most 4 entries are 1, and exactly 4 in some share. `later_pattern`: in each aligned share of 1 x 8 entries held by one device, at most 4 entries are 1, and exactly 4 in some share.
All inputs are finite; a program needn't handle non-finite values.
Results may differ from the reference program's by a relative error of at most 0.0003.
Values may be sent and summed in bfloat16 or wider, within the bound.
A program may use at most 256 MiB of HBM per device.

```python
import jax
import jax.numpy as jnp
from jax import lax

BLK = 128
ROWB_DEV = 4
COLB_DEV = 8
KB_DEV = 1
TK = 48
ROWS = 32
COLS = 32
KB = 8
KA_DEV = 2
N_ROW = 8
N_COL = 4


def draw_pattern(key, shard_rows, shard_cols, grid_rows, grid_cols):
    count_each = shard_rows * shard_cols
    capacity = max(1, count_each // 2)
    shards = grid_rows * grid_cols
    key_count, key_full, key_order = jax.random.split(key, 3)
    counts = jax.random.randint(key_count, (shards,), (capacity + 1) // 2, capacity + 1)
    chosen = jax.random.randint(key_full, (), 0, shards)
    counts = jnp.where(jnp.arange(shards) == chosen, capacity, counts)
    scores = jax.random.randint(key_order, (shards, count_each), 0, 1 << 20) * count_each + jnp.arange(count_each)[None, :]
    rank_order = jnp.argsort(jnp.argsort(scores, axis=1), axis=1)
    live_flags = (rank_order < counts[:, None]).astype(jnp.int32)
    arranged = live_flags.reshape(grid_rows, grid_cols, shard_rows, shard_cols).transpose(0, 2, 1, 3)
    return arranged.reshape(grid_rows * shard_rows, grid_cols * shard_cols)


def draw_earlier_pattern(key, part):
    return draw_pattern(jax.random.fold_in(key, 11), ROWB_DEV, KA_DEV, N_ROW, N_COL)


def draw_later_pattern(key, part):
    return draw_pattern(jax.random.fold_in(key, 23), KB_DEV, COLB_DEV, N_ROW, N_COL)


def with_ends(result, own_key, low, high):
    longest = result.shape.index(max(result.shape))
    spots = []
    for shift in (0, 1):
        where = [jax.random.randint(jax.random.fold_in(own_key, axis), (), 0, length) for axis, length in enumerate(result.shape)]
        where[longest] = (where[longest] + shift) % result.shape[longest]
        spots.append(tuple(where))
    return result.at[spots[0]].set(low).at[spots[1]].set(high)


def steps_of(own_key, extent, cuts, low, top_value):
    level = 1.0
    for dim, parts in cuts:
        steps = jax.random.uniform(jax.random.fold_in(jax.random.fold_in(own_key, 6), dim), (parts,), jnp.float32, low / len(cuts), top_value / len(cuts))
        level = level * jnp.repeat(jnp.exp(steps), extent[dim] // parts).reshape((-1,) + (1,) * (len(extent) - 1 - dim))
    return level


def normal_values(rng, extent, deviation, reach, cuts=(), held_as=jnp.bfloat16):
    level = steps_of(rng, extent, cuts, -0.22, 0.18) if cuts else 1.0
    values = jax.random.normal(rng, extent, jnp.float32) * deviation * level
    return jnp.minimum(jnp.maximum(values, -reach), reach).astype(held_as)


def setup_inputs(seed: int = 0) -> dict:
    streams_of = jax.random.split(jax.random.key(seed), 6)
    return {
        "earlier_blocks": normal_values(streams_of[0], (ROWS, KB, BLK, BLK), BLK ** -0.5, 0.5, ((0, 8), (1, 4))),
        "later_blocks": normal_values(streams_of[1], (KB, COLS, BLK, BLK), 1.0, 6.0, ((0, 8), (1, 4))),
        "earlier_pattern": draw_earlier_pattern(jax.random.fold_in(streams_of[5], 71), 0),
        "later_pattern": draw_later_pattern(jax.random.fold_in(streams_of[5], 71), 0),
        "triples": with_ends(jax.random.randint(streams_of[4], (ROWS, COLS, TK), 0, KB), jax.random.fold_in(streams_of[4], 1), 0, KB - 1).astype(jnp.int32),
    }


def reference(earlier_blocks, later_blocks, earlier_pattern, later_pattern, triples):
    earlier_live = earlier_blocks * earlier_pattern[:, :, None, None].astype(jnp.bfloat16)
    later_live = later_blocks * later_pattern[:, :, None, None].astype(jnp.bfloat16)
    col_numbers = jnp.arange(later_live.shape[1], dtype=jnp.int32)[:, None]

    def one_row(inputs):
        row_blocks, row_triples = inputs
        earlier_pick = row_blocks[row_triples].astype(jnp.float32)
        later_pick = later_live[row_triples, col_numbers].astype(jnp.float32)
        return jnp.einsum("jtab,jtbc->jac", earlier_pick, later_pick, precision=lax.Precision.HIGHEST)

    return lax.map(one_row, (earlier_live, triples))
```

```python
import functools

import jax
import jax.numpy as jnp
from jax import lax
from jax.experimental import pallas as pl
from jax.experimental.pallas import tpu as pltpu
from jax.sharding import PartitionSpec as P

MESH = pl.DeviceIdType.MESH
LANES = 128
HALVES = 2


def ranks(live):
    out, rank = [], jnp.int32(0)
    for flag in live:
        out.append(rank)
        rank = rank + flag
    return out


def entry_of_slot(live, rank, slot):
    entry = jnp.int32(0)
    for number, (flag, place) in enumerate(zip(live, rank)):
        entry = entry + jnp.where(jnp.logical_and(flag == 1, place == slot), number, 0)
    return entry


def kernel(
    n_row, n_col,
    e_hbm, l_hbm, ep_hbm, lp_hbm, t_hbm,
    out_ref,
    e_ref, l_ref, t_ref, ep_ref, lp_ref,
    eg_ref, lg_ref, em_ref, lm_ref, cnt_ref, weight_ref, p_ref,
    fetch_sem, count_sem,
    send_e, recv_e, send_own, recv_own, send_far, recv_far, send_core, recv_core,
):
    rows, early_ka, side, _ = e_ref.shape
    cols = l_ref.shape[1]
    slots_e, slots_l = eg_ref.shape[1], lg_ref.shape[1]
    row, col = lax.axis_index("row"), lax.axis_index("col")
    core, chip = lax.rem(row, 2), row // 2
    chips = n_row // 2
    relay = chips == 4
    has_right = col < n_col - 1
    has_left = col > 0

    fetches = [
        pltpu.make_async_copy(src, dst, fetch_sem.at[n])
        for n, (src, dst) in enumerate((
            (ep_hbm, ep_ref), (lp_hbm, lp_ref), (e_hbm, e_ref), (l_hbm, l_ref), (t_hbm, t_ref),
        ))
    ]
    for copy in fetches:
        copy.start()

    partner = (row + 1 - 2 * core, col)
    if relay:
        beside = chip + 1 - 2 * lax.rem(chip, 2)
        across = chip + 2 - 4 * (chip // 2)
        near = core * across + (1 - core) * beside
        other = core * beside + (1 - core) * across
        facing = 3 - chip
        direct = [near, other]
        chip_of = [chip, near, other, facing]
    else:
        direct = [lax.rem(chip + d, chips) for d in range(1, chips)]
        chip_of = [chip] + [lax.rem(chip + chips - d, chips) for d in range(1, chips)]
    to_chip = [(2 * there + core, col) for there in direct]
    messages = len(chip_of)

    barrier = pltpu.get_barrier_semaphore()
    for there, step in ((has_left, -1), (has_right, 1)):
        @pl.when(there)
        def _():
            pl.semaphore_signal(
                barrier, inc=1, device_id=(row, col + step), device_id_type=MESH
            )
    for device in to_chip + [partner]:
        pl.semaphore_signal(barrier, inc=1, device_id=device, device_id_type=MESH)

    fetches[0].wait()
    order = [(a, b) for b in range(early_ka) for a in range(rows)]
    live = [ep_ref[b, a] for a, b in order]
    rank = ranks(live)
    for n, (flag, place) in enumerate(zip(live, rank)):
        em_ref[col, 0, n] = jnp.where(flag == 1, place, slots_e)
    picks_e = [entry_of_slot(live, rank, s) for s in range(slots_e)]
    for s, entry in enumerate(picks_e):
        em_ref[col, 0, len(order) + s] = entry // rows
    fetches[1].wait()
    live = [lp_ref[0, j] for j in range(cols)]
    rank = ranks(live)
    for n, (flag, place) in enumerate(zip(live, rank)):
        lm_ref[row, 0, n] = jnp.where(flag == 1, place, slots_l)
    picks_l = [entry_of_slot(live, rank, s) for s in range(slots_l)]

    def remote(src, dst, send, recv, device):
        return pltpu.make_async_remote_copy(
            src_ref=src, dst_ref=dst, send_sem=send, recv_sem=recv,
            device_id=device, device_id_type=MESH,
        )

    def along(way, hop, chunk):
        step = 1 - 2 * way
        source = col - step * hop
        ref = em_ref.at[source] if chunk == 0 else eg_ref.at[source, chunk - 1]
        return remote(
            ref, ref, send_e.at[way, hop, chunk], recv_e.at[way, hop, chunk], (row, col + step)
        )

    def sends(way, hop):
        if way == 0:
            return jnp.logical_and(has_right, col >= hop)
        return jnp.logical_and(has_left, col + hop < n_col)

    def receives(way, hop):
        return col >= hop + 1 if way == 0 else col + hop + 1 < n_col

    hops = range(n_col - 1)
    chunks = range(slots_e + 1)

    half = slots_l // HALVES

    def later_parts(source, sems):
        send, recv = sems
        parts = [(lm_ref.at[source], send.at[0], recv.at[0])]
        for n in range(HALVES):
            ref = lg_ref.at[source, pl.ds(n * half, half)]
            parts.append((ref, send.at[n + 1], recv.at[n + 1]))
        return parts

    def later(source, sems, device):
        return [remote(ref, ref, s, r, device) for ref, s, r in later_parts(source, sems)]

    fetches[2].wait()
    for s, entry in enumerate(picks_e):
        eg_ref[col, s] = e_ref[lax.rem(entry, rows), entry // rows]
    fetches[3].wait()
    for s, entry in enumerate(picks_l):
        lg_ref[row, s] = l_ref[0, entry]
    ends = has_right.astype(jnp.int32) + has_left.astype(jnp.int32)
    pl.semaphore_wait(barrier, len(to_chip) + 1 + ends)

    def sem_of(pair, n):
        return pair[0].at[n], pair[1].at[n]

    own_out = [
        later(row, sem_of((send_own, recv_own), n), device) for n, device in enumerate(to_chip)
    ]
    core_out = [
        later(2 * there + core, sem_of((send_core, recv_core), n), partner)
        for n, there in enumerate(chip_of)
    ]
    if relay:
        far_out = later(2 * near + core, (send_far, recv_far), to_chip[1])
    for chunk in chunks:
        for way in range(2):
            @pl.when(sends(way, 0))
            def _():
                along(way, 0, chunk).start()
        for group in own_out:
            if chunk <= HALVES:
                group[chunk].start()
    for copy in core_out[0]:
        copy.start()

    for s in range(slots_e + 1):
        p_ref[s, slots_l] = jnp.zeros((side, side), jnp.float32)
    for u in range(slots_l):
        p_ref[slots_e, u] = jnp.zeros((side, side), jnp.float32)
    fetches[4].wait()
    middle = n_row
    lane = lax.broadcasted_iota(jnp.int32, (cols, LANES), 1)
    for i in range(rows):
        numbers = t_ref[i]
        counts = jnp.zeros((cols, LANES), jnp.float32)
        for k in range(middle):
            hits = jnp.sum(jnp.where(numbers == k, 1.0, 0.0), axis=1, keepdims=True)
            counts = jnp.where(lane == k, hits, counts)
        cnt_ref[i * cols:(i + 1) * cols, :] = counts
    to_scalar = pltpu.make_async_copy(cnt_ref, weight_ref, count_sem)
    to_scalar.start()

    def land(hop, chunk):
        for way in range(2):
            @pl.when(receives(way, hop))
            def _():
                along(way, hop, chunk).wait_recv()
            if hop + 1 < n_col - 1:
                @pl.when(sends(way, hop + 1))
                def _():
                    along(way, hop + 1, chunk).start()

    def arrive(message, part):
        if relay:
            if message == 3:
                later(2 * facing + core, (send_far, recv_far), to_chip[1])[part].wait_recv()
            else:
                own_out[message - 1][part].wait_recv()
                if message == 1:
                    far_out[part].start()
        else:
            own_out[message - 1][part].wait_recv()
        core_out[message][part].start()

    early = [(hop, chunk) for hop in hops[:-1] for chunk in chunks]
    rest = [(m, part) for m in range(1, messages) for part in range(HALVES + 1)]
    if relay:
        rest = [(m, part) for part in range(HALVES + 1) for m in (1, 2)]
        rest += [(3, part) for part in range(HALVES + 1)]
    stride = max(1, -(-len(early) // max(1, len(rest))))
    step = 0
    while early or rest:
        if early:
            land(*early.pop(0))
        if rest and step % stride == stride - 1 or not early:
            if rest:
                arrive(*rest.pop(0))
        step += 1
    for group in core_out:
        for copy in group:
            copy.wait_recv()
    to_scalar.wait()

    def form(source, s):
        k = source * early_ka + em_ref[source, 0, len(order) + s]
        wide = jnp.concatenate([lg_ref[k, u] for u in range(slots_l)], axis=1)
        product = jnp.dot(eg_ref[source, s], wide, preferred_element_type=jnp.float32)
        for u in range(slots_l):
            p_ref[s, u] = product[:, u * side:(u + 1) * side]

    def spread(source, fresh):
        def one_row(i, carry):
            for j in range(cols):
                total = None if fresh else out_ref[i, j]
                for b in range(early_ka):
                    k = source * early_ka + b
                    s = em_ref[source, 0, b * rows + i]
                    u = lm_ref[k, 0, j]
                    term = weight_ref[i * cols + j, k] * p_ref[s, u]
                    total = term if total is None else total + term
                out_ref[i, j] = total
            return carry
        lax.fori_loop(0, rows, one_row, 0)

    for s in range(slots_e):
        form(col, s)
    spread(col, True)

    def one_column(source, carry):
        inside = jnp.logical_and(source < col + n_col - 1, source > col - n_col + 1)
        @pl.when(jnp.logical_and(source != col, inside))
        def _():
            for s in range(slots_e):
                form(source, s)
            spread(source, False)
        return carry

    lax.fori_loop(0, n_col, one_column, 0)

    last = n_col - 2
    @pl.when(jnp.logical_or(receives(0, last), receives(1, last)))
    def _():
        source = n_col - 1 - col
        for chunk in chunks:
            land(last, chunk)
            if chunk:
                form(source, chunk - 1)
        spread(source, False)

    for group in own_out + core_out:
        for copy in group:
            copy.wait_send()
    if relay:
        for copy in far_out:
            copy.wait_send()
    for hop in hops:
        for way in range(2):
            @pl.when(sends(way, hop))
            def _():
                for chunk in chunks:
                    along(way, hop, chunk).wait_send()


def on_device(n_row, n_col, earlier_blocks, later_blocks, earlier_pattern, later_pattern, triples):
    rows, early_ka, side, _ = earlier_blocks.shape
    late_kb, cols = later_blocks.shape[:2]
    assert late_kb == 1
    slots_e = max(1, rows * early_ka // 2)
    slots_l = max(1, late_kb * cols // 2)
    chips = n_row // 2
    direct = 2 if chips == 4 else chips - 1
    parts = HALVES + 1
    vmem = pl.BlockSpec(memory_space=pltpu.VMEM)
    hbm = pl.BlockSpec(memory_space=pltpu.HBM)
    block = jnp.bfloat16
    dma = pltpu.SemaphoreType.DMA
    return pl.pallas_call(
        functools.partial(kernel, n_row, n_col),
        out_shape=jax.ShapeDtypeStruct((rows, cols, side, side), jnp.float32),
        in_specs=[hbm] * 5,
        out_specs=vmem,
        scratch_shapes=[
            pltpu.VMEM(earlier_blocks.shape, block),
            pltpu.VMEM(later_blocks.shape, block),
            pltpu.VMEM(triples.shape, jnp.int32),
            pltpu.SMEM((early_ka, rows), jnp.int32),
            pltpu.SMEM(later_pattern.shape, jnp.int32),
            pltpu.VMEM((n_col, slots_e, side, side), block),
            pltpu.VMEM((n_row, slots_l, side, side), block),
            pltpu.SMEM((n_col, 1, LANES), jnp.int32),
            pltpu.SMEM((n_row, 1, LANES), jnp.int32),
            pltpu.VMEM((rows * cols, LANES), jnp.float32),
            pltpu.SMEM((rows * cols, LANES), jnp.float32),
            pltpu.VMEM((slots_e + 1, slots_l + 1, side, side), jnp.float32),
            dma((5,)),
            dma(()),
            dma((2, n_col, slots_e + 1)),
            dma((2, n_col, slots_e + 1)),
            dma((direct, parts)),
            dma((direct, parts)),
            dma((parts,)),
            dma((parts,)),
            dma((chips, parts)),
            dma((chips, parts)),
        ],
        compiler_params=pltpu.CompilerParams(
            collective_id=0, has_side_effects=True, vmem_limit_bytes=32 << 20
        ),
        name="gather_compose",
    )(*(
        pltpu.with_memory_space_constraint(x, pltpu.HBM)
        for x in (earlier_blocks, later_blocks, earlier_pattern.T, later_pattern, triples)
    ))


def solution(mesh):
    return jax.shard_map(
        functools.partial(on_device, mesh.shape["row"], mesh.shape["col"]),
        mesh=mesh,
        in_specs=(
            P("row", "col", None, None),
            P("row", "col", None, None),
            P("row", "col"),
            P("row", "col"),
            P("row", "col", None),
        ),
        out_specs=P("row", "col", None, None),
        check_vma=False,
    )
```

```python
import functools

import jax
import jax.numpy as jnp
from jax import lax
from jax.experimental import pallas as pl
from jax.experimental.pallas import tpu as pltpu
from jax.sharding import PartitionSpec as P

MESH = pl.DeviceIdType.MESH
LANES = 128
HALVES = 2


def ranks(live):
    out, rank = [], jnp.int32(0)
    for flag in live:
        out.append(rank)
        rank = rank + flag
    return out


def entry_of_slot(live, rank, slot):
    entry = jnp.int32(0)
    for number, (flag, place) in enumerate(zip(live, rank)):
        entry = entry + jnp.where(jnp.logical_and(flag == 1, place == slot), number, 0)
    return entry


def kernel(
    n_row, n_col,
    e_hbm, l_hbm, ep_hbm, lp_hbm, t_hbm,
    out_ref,
    e_ref, l_ref, t_ref, ep_ref, lp_ref,
    eg_ref, lg_ref, em_ref, lm_ref, cnt_ref, weight_ref, p_ref,
    fetch_sem, count_sem,
    send_e, recv_e, send_on, send_own, recv_own, send_far, recv_far, send_core, recv_core,
):
    rows, early_ka, side, _ = e_ref.shape
    cols = l_ref.shape[1]
    slots_e, slots_l = eg_ref.shape[1], lg_ref.shape[1]
    row, col = lax.axis_index("row"), lax.axis_index("col")
    core, chip = lax.rem(row, 2), row // 2
    chips = n_row // 2
    relay = chips == 4

    fetches = [
        pltpu.make_async_copy(src, dst, fetch_sem.at[n])
        for n, (src, dst) in enumerate((
            (ep_hbm, ep_ref), (lp_hbm, lp_ref), (e_hbm, e_ref), (l_hbm, l_ref), (t_hbm, t_ref),
        ))
    ]
    for copy in fetches:
        copy.start()

    partner = (row + 1 - 2 * core, col)
    if relay:
        beside = chip + 1 - 2 * lax.rem(chip, 2)
        across = chip + 2 - 4 * (chip // 2)
        near = core * across + (1 - core) * beside
        other = core * beside + (1 - core) * across
        facing = 3 - chip
        direct = [near, other]
        chip_of = [chip, near, other, facing]
    else:
        direct = [lax.rem(chip + d, chips) for d in range(1, chips)]
        chip_of = [chip] + [lax.rem(chip + chips - d, chips) for d in range(1, chips)]
    to_chip = [(2 * there + core, col) for there in direct]
    messages = len(chip_of)

    def direct_e(source, target):
        ends = jnp.logical_or(
            jnp.logical_and(target == 0, source >= 2),
            jnp.logical_and(target == n_col - 1, source <= n_col - 3),
        )
        inside = jnp.logical_and(target >= 0, target < n_col)
        return jnp.logical_and(inside, jnp.logical_not(ends))

    def passes(source):
        left = jnp.logical_and(col == 1, source >= 2)
        return jnp.logical_or(left, jnp.logical_and(col == n_col - 2, source <= n_col - 3))

    offsets = [sign * d for d in range(n_col - 1, 0, -1) for sign in (-1, 1)]

    barrier = pltpu.get_barrier_semaphore()
    expected = jnp.int32(len(to_chip) + 1)
    for offset in offsets:
        source = col + offset
        inside = jnp.logical_and(source >= 0, source < n_col)
        @pl.when(jnp.logical_and(inside, direct_e(source, col)))
        def _():
            pl.semaphore_signal(
                barrier, inc=1, device_id=(row, source), device_id_type=MESH
            )
        expected = expected + direct_e(col, source).astype(jnp.int32)
    for device in to_chip + [partner]:
        pl.semaphore_signal(barrier, inc=1, device_id=device, device_id_type=MESH)

    def remote(src, dst, send, recv, device):
        return pltpu.make_async_remote_copy(
            src_ref=src, dst_ref=dst, send_sem=send, recv_sem=recv,
            device_id=device, device_id_type=MESH,
        )

    chunks = range(slots_e + 1)

    def earlier(source, chunk, target, send):
        ref = em_ref.at[source] if chunk == 0 else eg_ref.at[source, chunk - 1]
        return remote(ref, ref, send.at[chunk], recv_e.at[source, chunk], (row, target))

    half = slots_l // HALVES
    parts = range(HALVES + 1)

    def later(source, part, send, recv, device):
        ref = lm_ref.at[source] if part == 0 else lg_ref.at[source, pl.ds((part - 1) * half, half)]
        return remote(ref, ref, send.at[part], recv.at[part], device)

    def own_out(n, part):
        return later(row, part, send_own.at[n], recv_own.at[n], to_chip[n])

    def core_out(n, part):
        return later(2 * chip_of[n] + core, part, send_core.at[n], recv_core.at[n], partner)

    def far_out(part):
        return later(2 * near + core, part, send_far, recv_far, to_chip[1])

    order = [(a, b) for b in range(early_ka) for a in range(rows)]
    fetches[0].wait()
    live = [ep_ref[b, a] for a, b in order]
    rank = ranks(live)
    picks_e = [entry_of_slot(live, rank, s) for s in range(slots_e)]
    for n, (flag, place) in enumerate(zip(live, rank)):
        em_ref[col, 0, n] = jnp.where(flag == 1, place, slots_e)
    for s, entry in enumerate(picks_e):
        em_ref[col, 0, len(order) + s] = entry // rows
    fetches[2].wait()
    for s, entry in enumerate(picks_e):
        eg_ref[col, s] = e_ref[lax.rem(entry, rows), entry // rows]
    pl.semaphore_wait(barrier, expected)
    for offset in offsets:
        target = col + offset
        @pl.when(direct_e(col, target))
        def _():
            for chunk in chunks:
                earlier(col, chunk, target, send_e.at[target]).start()

    fetches[1].wait()
    live = [lp_ref[0, j] for j in range(cols)]
    rank = ranks(live)
    picks_l = [entry_of_slot(live, rank, s) for s in range(slots_l)]
    for n, (flag, place) in enumerate(zip(live, rank)):
        lm_ref[row, 0, n] = jnp.where(flag == 1, place, slots_l)
    fetches[3].wait()
    for s, entry in enumerate(picks_l):
        lg_ref[row, s] = l_ref[0, entry]
    for part in parts:
        for n in range(len(to_chip)):
            own_out(n, part).start()
    for part in parts:
        core_out(0, part).start()

    for s in range(slots_e + 1):
        p_ref[s, slots_l] = jnp.zeros((side, side), jnp.float32)
    for u in range(slots_l):
        p_ref[slots_e, u] = jnp.zeros((side, side), jnp.float32)
    fetches[4].wait()
    middle = n_row
    lane = lax.broadcasted_iota(jnp.int32, (cols, LANES), 1)
    for i in range(rows):
        numbers = t_ref[i]
        counts = jnp.zeros((cols, LANES), jnp.float32)
        for k in range(middle):
            hits = jnp.sum(jnp.where(numbers == k, 1.0, 0.0), axis=1, keepdims=True)
            counts = jnp.where(lane == k, hits, counts)
        cnt_ref[i * cols:(i + 1) * cols, :] = counts
    to_scalar = pltpu.make_async_copy(cnt_ref, weight_ref, count_sem)
    to_scalar.start()

    def await_e(source, chunk):
        earlier(source, chunk, col, send_e.at[source]).wait_recv()

    def hand_on(source, chunk, target):
        await_e(source, chunk)
        earlier(source, chunk, target, send_on.at[source]).start()

    def both_ways(distance, chunk):
        if distance >= n_col - 1:
            return
        @pl.when(col == 1)
        def _():
            hand_on(1 + distance, chunk, 0)
        @pl.when(col == n_col - 2)
        def _():
            hand_on(n_col - 2 - distance, chunk, n_col - 1)

    def arrive(message, part):
        if relay and message == 3:
            later(2 * facing + core, part, send_far, recv_far, to_chip[1]).wait_recv()
        else:
            own_out(message - 1, part).wait_recv()
            if relay and message == 1:
                far_out(part).start()
        core_out(message, part).start()

    if relay:
        arrivals = [(m, part) for part in parts for m in (1, 2)] + [(3, part) for part in parts]
    else:
        arrivals = [(m, part) for m in range(1, messages) for part in parts]
    onward = [(d, chunk) for d in range(1, n_col - 1) for chunk in chunks]
    slots = len(arrivals)
    for n in range(max(len(onward), slots)):
        if n < len(onward):
            both_ways(*onward[n])
        if n < slots:
            arrive(*arrivals[n])
    for n in range(messages):
        for part in parts:
            core_out(n, part).wait_recv()
    to_scalar.wait()

    def form(source, s):
        k = source * early_ka + em_ref[source, 0, len(order) + s]
        wide = jnp.concatenate([lg_ref[k, u] for u in range(slots_l)], axis=1)
        product = jnp.dot(eg_ref[source, s], wide, preferred_element_type=jnp.float32)
        for u in range(slots_l):
            p_ref[s, u] = product[:, u * side:(u + 1) * side]

    def spread(source, fresh):
        def one_row(i, carry):
            for j in range(cols):
                total = None if fresh else out_ref[i, j]
                for b in range(early_ka):
                    k = source * early_ka + b
                    s = em_ref[source, 0, b * rows + i]
                    u = lm_ref[k, 0, j]
                    term = weight_ref[i * cols + j, k] * p_ref[s, u]
                    total = term if total is None else total + term
                out_ref[i, j] = total
            return carry
        lax.fori_loop(0, rows, one_row, 0)

    for s in range(slots_e):
        form(col, s)
    spread(col, True)

    at_end = jnp.logical_or(col == 0, col == n_col - 1)
    last = n_col - 1 - col

    def one_column(number, carry):
        source = jnp.where(col < n_col // 2, number, n_col - 1 - number)
        held_back = jnp.logical_and(at_end, source == last)
        @pl.when(jnp.logical_and(source != col, jnp.logical_not(held_back)))
        def _():
            @pl.when(jnp.logical_not(passes(source)))
            def _():
                for chunk in chunks:
                    await_e(source, chunk)
            for s in range(slots_e):
                form(source, s)
            spread(source, False)
        return carry

    lax.fori_loop(0, n_col, one_column, 0)

    @pl.when(at_end)
    def _():
        for chunk in chunks:
            await_e(last, chunk)
            if chunk:
                form(last, chunk - 1)
        spread(last, False)

    for part in parts:
        for n in range(len(to_chip)):
            own_out(n, part).wait_send()
        for n in range(messages):
            core_out(n, part).wait_send()
        if relay:
            far_out(part).wait_send()
    for offset in offsets:
        target = col + offset
        @pl.when(direct_e(col, target))
        def _():
            for chunk in chunks:
                earlier(col, chunk, target, send_e.at[target]).wait_send()
    for source in range(n_col):
        for end, middle_col in ((0, 1), (n_col - 1, n_col - 2)):
            if abs(source - end) >= 2:
                @pl.when(col == middle_col)
                def _():
                    for chunk in chunks:
                        earlier(source, chunk, end, send_on.at[source]).wait_send()


def on_device(n_row, n_col, earlier_blocks, later_blocks, earlier_pattern, later_pattern, triples):
    rows, early_ka, side, _ = earlier_blocks.shape
    late_kb, cols = later_blocks.shape[:2]
    assert late_kb == 1
    slots_e = max(1, rows * early_ka // 2)
    slots_l = max(1, late_kb * cols // 2)
    chips = n_row // 2
    direct = 2 if chips == 4 else chips - 1
    parts = HALVES + 1
    vmem = pl.BlockSpec(memory_space=pltpu.VMEM)
    hbm = pl.BlockSpec(memory_space=pltpu.HBM)
    block = jnp.bfloat16
    dma = pltpu.SemaphoreType.DMA
    return pl.pallas_call(
        functools.partial(kernel, n_row, n_col),
        out_shape=jax.ShapeDtypeStruct((rows, cols, side, side), jnp.float32),
        in_specs=[hbm] * 5,
        out_specs=vmem,
        scratch_shapes=[
            pltpu.VMEM(earlier_blocks.shape, block),
            pltpu.VMEM(later_blocks.shape, block),
            pltpu.VMEM(triples.shape, jnp.int32),
            pltpu.SMEM((early_ka, rows), jnp.int32),
            pltpu.SMEM(later_pattern.shape, jnp.int32),
            pltpu.VMEM((n_col, slots_e, side, side), block),
            pltpu.VMEM((n_row, slots_l, side, side), block),
            pltpu.SMEM((n_col, 1, LANES), jnp.int32),
            pltpu.SMEM((n_row, 1, LANES), jnp.int32),
            pltpu.VMEM((rows * cols, LANES), jnp.float32),
            pltpu.SMEM((rows * cols, LANES), jnp.float32),
            pltpu.VMEM((slots_e + 1, slots_l + 1, side, side), jnp.float32),
            dma((5,)),
            dma(()),
            dma((n_col, slots_e + 1)),
            dma((n_col, slots_e + 1)),
            dma((n_col, slots_e + 1)),
            dma((direct, parts)),
            dma((direct, parts)),
            dma((parts,)),
            dma((parts,)),
            dma((chips, parts)),
            dma((chips, parts)),
        ],
        compiler_params=pltpu.CompilerParams(
            collective_id=0, has_side_effects=True, vmem_limit_bytes=32 << 20
        ),
        name="gather_compose",
    )(*(
        pltpu.with_memory_space_constraint(x, pltpu.HBM)
        for x in (earlier_blocks, later_blocks, earlier_pattern.T, later_pattern, triples)
    ))


def solution(mesh):
    return jax.shard_map(
        functools.partial(on_device, mesh.shape["row"], mesh.shape["col"]),
        mesh=mesh,
        in_specs=(
            P("row", "col", None, None),
            P("row", "col", None, None),
            P("row", "col"),
            P("row", "col"),
            P("row", "col", None),
        ),
        out_specs=P("row", "col", None, None),
        check_vma=False,
    )
```

```python
import functools

import jax
import jax.numpy as jnp
from jax import lax
from jax.experimental import pallas as pl
from jax.experimental.pallas import tpu as pltpu
from jax.sharding import PartitionSpec as P

MESH = pl.DeviceIdType.MESH
LANES = 128
HALVES = 2


def ranks(live):
    out, rank = [], jnp.int32(0)
    for flag in live:
        out.append(rank)
        rank = rank + flag
    return out


def entry_of_slot(live, rank, slot):
    entry = jnp.int32(0)
    for number, (flag, place) in enumerate(zip(live, rank)):
        entry = entry + jnp.where(jnp.logical_and(flag == 1, place == slot), number, 0)
    return entry


def kernel(
    n_row, n_col,
    e_hbm, l_hbm, ep_hbm, lp_hbm, t_hbm,
    out_any,
    e_ref, l_ref, t_ref, ep_ref, lp_ref,
    eg_ref, lg_ref, em_ref, lm_ref, cnt_ref, weight_ref, p_ref, out_ref,
    fetch_sem, count_sem,
    send_e, recv_e, send_on, send_own, recv_own, send_core, recv_core, out_sem,
):
    rows, early_ka, side, _ = e_ref.shape
    cols = l_ref.shape[1]
    slots_e, slots_l = eg_ref.shape[1], lg_ref.shape[1]
    row, col = lax.axis_index("row"), lax.axis_index("col")
    core, chip = lax.rem(row, 2), row // 2
    chips = n_row // 2

    fetches = [
        pltpu.make_async_copy(src, dst, fetch_sem.at[n])
        for n, (src, dst) in enumerate((
            (ep_hbm, ep_ref), (lp_hbm, lp_ref), (e_hbm, e_ref), (l_hbm, l_ref), (t_hbm, t_ref),
        ))
    ]
    for copy in fetches:
        copy.start()

    partner = (row + 1 - 2 * core, col)
    if chips & (chips - 1) == 0:
        bits = range(chips.bit_length() - 1)
        steps = sorted(range(1, chips), key=lambda m: (-m.bit_count(), -m))
        def moved(m):
            digits = [lax.rem(chip // 2**b, 2) for b in bits]
            return sum((1 - v if m >> b & 1 else v) * 2**b for b, v in zip(bits, digits))
        direct = [moved(m) for m in steps]
        chip_of = [chip] + direct
    else:
        direct = [lax.rem(chip + d, chips) for d in range(1, chips)]
        chip_of = [chip] + [lax.rem(chip + chips - d, chips) for d in range(1, chips)]
    to_chip = [(2 * there + core, col) for there in direct]
    messages = len(chip_of)

    def direct_e(source, target):
        ends = jnp.logical_or(
            jnp.logical_and(target == 0, source >= 2),
            jnp.logical_and(target == n_col - 1, source <= n_col - 3),
        )
        inside = jnp.logical_and(target >= 0, target < n_col)
        return jnp.logical_and(inside, jnp.logical_not(ends))

    def passes(source):
        left = jnp.logical_and(col == 1, source >= 2)
        return jnp.logical_or(left, jnp.logical_and(col == n_col - 2, source <= n_col - 3))

    offsets = [sign * d for d in range(1, n_col) for sign in (-1, 1)]

    barrier = pltpu.get_barrier_semaphore()
    expected = jnp.int32(len(to_chip) + 1)
    for offset in offsets:
        source = col + offset
        inside = jnp.logical_and(source >= 0, source < n_col)
        @pl.when(jnp.logical_and(inside, direct_e(source, col)))
        def _():
            pl.semaphore_signal(
                barrier, inc=1, device_id=(row, source), device_id_type=MESH
            )
        expected = expected + direct_e(col, source).astype(jnp.int32)
    for device in to_chip + [partner]:
        pl.semaphore_signal(barrier, inc=1, device_id=device, device_id_type=MESH)

    def remote(src, dst, send, recv, device):
        return pltpu.make_async_remote_copy(
            src_ref=src, dst_ref=dst, send_sem=send, recv_sem=recv,
            device_id=device, device_id_type=MESH,
        )

    chunks = range(slots_e + 1)

    def earlier(source, chunk, target, send):
        ref = em_ref.at[source] if chunk == 0 else eg_ref.at[source, chunk - 1]
        return remote(ref, ref, send.at[chunk], recv_e.at[source, chunk], (row, target))

    half = slots_l // HALVES
    parts = range(HALVES + 1)

    def later(source, part, send, recv, device):
        ref = lm_ref.at[source] if part == 0 else lg_ref.at[source, pl.ds((part - 1) * half, half)]
        return remote(ref, ref, send.at[part], recv.at[part], device)

    def own_out(n, part):
        return later(row, part, send_own.at[n], recv_own.at[n], to_chip[n])

    def core_out(n, part):
        return later(2 * chip_of[n] + core, part, send_core.at[n], recv_core.at[n], partner)

    order = [(a, b) for b in range(early_ka) for a in range(rows)]
    fetches[0].wait()
    live = [ep_ref[b, a] for a, b in order]
    rank = ranks(live)
    picks_e = [entry_of_slot(live, rank, s) for s in range(slots_e)]
    for n, (flag, place) in enumerate(zip(live, rank)):
        em_ref[col, 0, n] = jnp.where(flag == 1, place, slots_e)
    for s, entry in enumerate(picks_e):
        em_ref[col, 0, len(order) + s] = entry // rows
    fetches[2].wait()
    for s, entry in enumerate(picks_e):
        eg_ref[col, s] = e_ref[lax.rem(entry, rows), entry // rows]
    pl.semaphore_wait(barrier, expected)
    for offset in offsets:
        target = col + offset
        @pl.when(direct_e(col, target))
        def _():
            for chunk in chunks:
                earlier(col, chunk, target, send_e.at[target]).start()

    fetches[1].wait()
    live = [lp_ref[0, j] for j in range(cols)]
    rank = ranks(live)
    picks_l = [entry_of_slot(live, rank, s) for s in range(slots_l)]
    for n, (flag, place) in enumerate(zip(live, rank)):
        lm_ref[row, 0, n] = jnp.where(flag == 1, place, slots_l)
    fetches[3].wait()
    for s, entry in enumerate(picks_l):
        lg_ref[row, s] = l_ref[0, entry]
    for n in range(len(to_chip)):
        for part in parts:
            own_out(n, part).start()
    for part in parts:
        core_out(0, part).start()

    for s in range(slots_e + 1):
        p_ref[s, slots_l] = jnp.zeros((side, side), jnp.float32)
    for u in range(slots_l):
        p_ref[slots_e, u] = jnp.zeros((side, side), jnp.float32)
    fetches[4].wait()
    middle = n_row
    lane = lax.broadcasted_iota(jnp.int32, (cols, LANES), 1)
    for i in range(rows):
        numbers = t_ref[i]
        counts = jnp.zeros((cols, LANES), jnp.float32)
        for k in range(middle):
            hits = jnp.sum(jnp.where(numbers == k, 1.0, 0.0), axis=1, keepdims=True)
            counts = jnp.where(lane == k, hits, counts)
        cnt_ref[i * cols:(i + 1) * cols, :] = counts
    to_scalar = pltpu.make_async_copy(cnt_ref, weight_ref, count_sem)
    to_scalar.start()

    def await_e(source, chunk):
        earlier(source, chunk, col, send_e.at[source]).wait_recv()

    def hand_on(source, chunk, target):
        await_e(source, chunk)
        earlier(source, chunk, target, send_on.at[source]).start()

    def both_ways(distance, chunk):
        if distance >= n_col - 1:
            return
        @pl.when(col == 1)
        def _():
            hand_on(1 + distance, chunk, 0)
        @pl.when(col == n_col - 2)
        def _():
            hand_on(n_col - 2 - distance, chunk, n_col - 1)

    def arrive(message, part):
        own_out(message - 1, part).wait_recv()
        core_out(message, part).start()

    nearest = list(range(messages - 1, 0, -1))
    for chunk in chunks:
        both_ways(1, chunk)
    if messages > 2:
        nearest[:2] = nearest[1::-1]
    for part in parts:
        arrive(nearest[0], part)
    for distance in range(2, n_col - 1):
        for chunk in chunks:
            both_ways(distance, chunk)
    for part in parts:
        for message in nearest[1:]:
            arrive(message, part)
    for n in range(messages):
        for part in parts:
            core_out(n, part).wait_recv()
    to_scalar.wait()

    def form(source, s):
        k = source * early_ka + em_ref[source, 0, len(order) + s]
        wide = jnp.concatenate([lg_ref[k, u] for u in range(slots_l)], axis=1)
        product = jnp.dot(eg_ref[source, s], wide, preferred_element_type=jnp.float32)
        for u in range(slots_l):
            p_ref[s, u] = product[:, u * side:(u + 1) * side]

    def leave(i):
        return pltpu.make_async_copy(out_ref.at[i], out_any.at[i], out_sem.at[i])

    def spread(source, fresh, final=False):
        def one_row(i, carry):
            for j in range(cols):
                total = None if fresh else out_ref[i, j]
                for b in range(early_ka):
                    k = source * early_ka + b
                    s = em_ref[source, 0, b * rows + i]
                    u = lm_ref[k, 0, j]
                    term = weight_ref[i * cols + j, k] * p_ref[s, u]
                    total = term if total is None else total + term
                out_ref[i, j] = total
            if final:
                leave(i).start()
            return carry
        lax.fori_loop(0, rows, one_row, 0)

    for s in range(slots_e):
        form(col, s)
    spread(col, True)

    at_end = jnp.logical_or(col == 0, col == n_col - 1)
    last = n_col - 1 - col

    def one_column(number, carry):
        source = jnp.where(col < n_col // 2, number, n_col - 1 - number)
        held_back = jnp.logical_and(at_end, source == last)
        @pl.when(jnp.logical_and(source != col, jnp.logical_not(held_back)))
        def _():
            @pl.when(jnp.logical_not(passes(source)))
            def _():
                for chunk in chunks:
                    await_e(source, chunk)
            for s in range(slots_e):
                form(source, s)
            spread(source, False)
        return carry

    lax.fori_loop(0, n_col, one_column, 0)

    @pl.when(at_end)
    def _():
        for chunk in chunks:
            await_e(last, chunk)
            if chunk:
                form(last, chunk - 1)
        spread(last, False, True)

    @pl.when(jnp.logical_not(at_end))
    def _():
        for i in range(rows):
            leave(i).start()

    for part in parts:
        for n in range(len(to_chip)):
            own_out(n, part).wait_send()
        for n in range(messages):
            core_out(n, part).wait_send()
    for offset in offsets:
        target = col + offset
        @pl.when(direct_e(col, target))
        def _():
            for chunk in chunks:
                earlier(col, chunk, target, send_e.at[target]).wait_send()
    for source in range(n_col):
        for end, middle_col in ((0, 1), (n_col - 1, n_col - 2)):
            if abs(source - end) >= 2:
                @pl.when(col == middle_col)
                def _():
                    for chunk in chunks:
                        earlier(source, chunk, end, send_on.at[source]).wait_send()
    for i in range(rows):
        leave(i).wait()


def on_device(n_row, n_col, earlier_blocks, later_blocks, earlier_pattern, later_pattern, triples):
    rows, early_ka, side, _ = earlier_blocks.shape
    late_kb, cols = later_blocks.shape[:2]
    assert late_kb == 1
    slots_e = max(1, rows * early_ka // 2)
    slots_l = max(1, late_kb * cols // 2)
    chips = n_row // 2
    direct = max(1, chips - 1)
    parts = HALVES + 1
    hbm = pl.BlockSpec(memory_space=pltpu.HBM)
    block = jnp.bfloat16
    dma = pltpu.SemaphoreType.DMA
    return pl.pallas_call(
        functools.partial(kernel, n_row, n_col),
        out_shape=jax.ShapeDtypeStruct((rows, cols, side, side), jnp.float32),
        in_specs=[hbm] * 5,
        out_specs=pl.BlockSpec(memory_space=pl.ANY),
        scratch_shapes=[
            pltpu.VMEM(earlier_blocks.shape, block),
            pltpu.VMEM(later_blocks.shape, block),
            pltpu.VMEM(triples.shape, jnp.int32),
            pltpu.SMEM((early_ka, rows), jnp.int32),
            pltpu.SMEM(later_pattern.shape, jnp.int32),
            pltpu.VMEM((n_col, slots_e, side, side), block),
            pltpu.VMEM((n_row, slots_l, side, side), block),
            pltpu.SMEM((n_col, 1, LANES), jnp.int32),
            pltpu.SMEM((n_row, 1, LANES), jnp.int32),
            pltpu.VMEM((rows * cols, LANES), jnp.float32),
            pltpu.SMEM((rows * cols, LANES), jnp.float32),
            pltpu.VMEM((slots_e + 1, slots_l + 1, side, side), jnp.float32),
            pltpu.VMEM((rows, cols, side, side), jnp.float32),
            dma((5,)),
            dma(()),
            dma((n_col, slots_e + 1)),
            dma((n_col, slots_e + 1)),
            dma((n_col, slots_e + 1)),
            dma((direct, parts)),
            dma((direct, parts)),
            dma((chips, parts)),
            dma((chips, parts)),
            dma((rows,)),
        ],
        compiler_params=pltpu.CompilerParams(
            collective_id=0, has_side_effects=True, vmem_limit_bytes=32 << 20
        ),
        name="gather_compose",
    )(*(
        pltpu.with_memory_space_constraint(x, pltpu.HBM)
        for x in (earlier_blocks, later_blocks, earlier_pattern.T, later_pattern, triples)
    ))


def solution(mesh):
    return jax.shard_map(
        functools.partial(on_device, mesh.shape["row"], mesh.shape["col"]),
        mesh=mesh,
        in_specs=(
            P("row", "col", None, None),
            P("row", "col", None, None),
            P("row", "col"),
            P("row", "col"),
            P("row", "col", None),
        ),
        out_specs=P("row", "col", None, None),
        check_vma=False,
    )
```

```python
import functools

import jax
import jax.numpy as jnp
from jax import lax
from jax.experimental import pallas as pl
from jax.experimental.pallas import tpu as pltpu
from jax.sharding import PartitionSpec as P

MESH = pl.DeviceIdType.MESH
LANES = 128
HALVES = 2


def ranks(live):
    out, rank = [], jnp.int32(0)
    for flag in live:
        out.append(rank)
        rank = rank + flag
    return out


def entry_of_slot(live, rank, slot):
    entry = jnp.int32(0)
    for number, (flag, place) in enumerate(zip(live, rank)):
        entry = entry + jnp.where(jnp.logical_and(flag == 1, place == slot), number, 0)
    return entry


def kernel(
    n_row, n_col,
    e_hbm, l_hbm, ep_hbm, lp_hbm, t_hbm,
    out_ref,
    e_ref, l_ref, t_ref, ep_ref, lp_ref,
    eg_ref, lg_ref, em_ref, lm_ref, cnt_ref, weight_ref, p_ref,
    fetch_sem, count_sem, ready_sem,
    send_e, recv_e, send_on, send_own, recv_own, send_core, recv_core,
):
    rows, early_ka, side, _ = e_ref.shape
    cols = l_ref.shape[1]
    slots_e, slots_l = eg_ref.shape[1], lg_ref.shape[1]
    row, col = lax.axis_index("row"), lax.axis_index("col")
    core, chip = lax.rem(row, 2), row // 2
    chips = n_row // 2
    bits = range(chips.bit_length() - 1)

    fetches = [
        pltpu.make_async_copy(src, dst, fetch_sem.at[n])
        for n, (src, dst) in enumerate((
            (ep_hbm, ep_ref), (lp_hbm, lp_ref), (e_hbm, e_ref), (l_hbm, l_ref), (t_hbm, t_ref),
        ))
    ]
    for copy in fetches:
        copy.start()

    def digits(number):
        return [lax.rem(number // 2**b, 2) for b in bits]

    def moved(m):
        return sum((1 - v if m >> b & 1 else v) * 2**b for b, v in zip(bits, digits(chip)))

    def apart(there):
        differ = [v + w - 2 * v * w for v, w in zip(digits(chip), digits(there))]
        return sum(v * 2**b for b, v in zip(bits, differ)), sum(differ)

    chip_of = [chip] + [moved(chips - n) for n in range(1, chips)]
    near = [n for n in range(chips - 1, 0, -1) if (chips - n).bit_count() == 1]
    far = [n for n in range(1, chips) if n not in near]
    vouched = chips == 4
    partner = (row + 1 - 2 * core, col)

    def place(n):
        return (2 * chip_of[n] + core, col)

    def direct_e(source, target):
        ends = jnp.logical_or(
            jnp.logical_and(target == 0, source >= 2),
            jnp.logical_and(target == n_col - 1, source <= n_col - 3),
        )
        inside = jnp.logical_and(target >= 0, target < n_col)
        return jnp.logical_and(inside, jnp.logical_not(ends))

    def passes(source):
        left = jnp.logical_and(col == 1, source >= 2)
        return jnp.logical_or(left, jnp.logical_and(col == n_col - 2, source <= n_col - 3))

    offsets = [sign * d for d in range(n_col - 1, 0, -1) for sign in (-1, 1)]

    barrier = pltpu.get_barrier_semaphore()
    greeted = [place(n) for n in (near if vouched else near + far)] + [partner]
    expected = jnp.int32(len(greeted))
    for offset in offsets:
        source = col + offset
        inside = jnp.logical_and(source >= 0, source < n_col)
        @pl.when(jnp.logical_and(inside, direct_e(source, col)))
        def _():
            pl.semaphore_signal(
                barrier, inc=1, device_id=(row, source), device_id_type=MESH
            )
        expected = expected + direct_e(col, source).astype(jnp.int32)
    for device in greeted:
        pl.semaphore_signal(barrier, inc=1, device_id=device, device_id_type=MESH)

    def remote(src, dst, send, recv, device):
        return pltpu.make_async_remote_copy(
            src_ref=src, dst_ref=dst, send_sem=send, recv_sem=recv,
            device_id=device, device_id_type=MESH,
        )

    chunks = range(slots_e + 1)

    def earlier(source, chunk, target, send):
        ref = em_ref.at[source] if chunk == 0 else eg_ref.at[source, chunk - 1]
        return remote(
            ref, ref, send.at[min(chunk, 1)], recv_e.at[source, chunk], (row, target)
        )

    half = slots_l // HALVES
    parts = range(HALVES + 1)

    def later_ref(source, part):
        if part == 0:
            return lm_ref.at[source]
        return lg_ref.at[source, pl.ds((part - 1) * half, half)]

    def own_out(n, part):
        ref = later_ref(row, part)
        return remote(ref, ref, send_own.at[min(part, 1)], recv_own.at[n - 1, part], place(n))

    def core_out(n, part):
        ref = later_ref(2 * chip_of[n] + core, part)
        kind = min(part, 1)
        return remote(ref, ref, send_core.at[kind], recv_core.at[n, kind], partner)

    def drain(ref, sem):
        pltpu.make_async_copy(ref, ref, sem).wait()

    order = [(a, b) for b in range(early_ka) for a in range(rows)]
    fetches[0].wait()
    live = [ep_ref[b, a] for a, b in order]
    rank = ranks(live)
    picks_e = [entry_of_slot(live, rank, s) for s in range(slots_e)]
    for n, (flag, spot) in enumerate(zip(live, rank)):
        em_ref[col, 0, n] = jnp.where(flag == 1, spot, slots_e)
    for s, entry in enumerate(picks_e):
        em_ref[col, 0, len(order) + s] = entry // rows
    fetches[2].wait()
    for s, entry in enumerate(picks_e):
        eg_ref[col, s] = e_ref[lax.rem(entry, rows), entry // rows]
    pl.semaphore_wait(barrier, expected)
    if vouched:
        pl.semaphore_signal(ready_sem, inc=1, device_id=place(near[0]), device_id_type=MESH)
    for offset in offsets:
        target = col + offset
        @pl.when(direct_e(col, target))
        def _():
            for chunk in chunks:
                earlier(col, chunk, target, send_e.at[target]).start()

    fetches[1].wait()
    live = [lp_ref[0, j] for j in range(cols)]
    rank = ranks(live)
    picks_l = [entry_of_slot(live, rank, s) for s in range(slots_l)]
    for n, (flag, spot) in enumerate(zip(live, rank)):
        lm_ref[row, 0, n] = jnp.where(flag == 1, spot, slots_l)
    fetches[3].wait()
    for s, entry in enumerate(picks_l):
        lg_ref[row, s] = l_ref[0, entry]
    for n in near:
        for part in parts:
            own_out(n, part).start()
    for part in parts:
        core_out(0, part).start()
    if vouched:
        pl.semaphore_wait(ready_sem, 1)
    for n in far:
        for part in parts:
            own_out(n, part).start()

    for s in range(slots_e + 1):
        p_ref[s, slots_l] = jnp.zeros((side, side), jnp.float32)
    for u in range(slots_l):
        p_ref[slots_e, u] = jnp.zeros((side, side), jnp.float32)
    fetches[4].wait()
    middle = n_row
    lane = lax.broadcasted_iota(jnp.int32, (cols, LANES), 1)
    for i in range(rows):
        numbers = t_ref[i]
        counts = jnp.zeros((cols, LANES), jnp.float32)
        for k in range(middle):
            hits = jnp.sum(jnp.where(numbers == k, 1.0, 0.0), axis=1, keepdims=True)
            counts = jnp.where(lane == k, hits, counts)
        cnt_ref[i * cols:(i + 1) * cols, :] = counts
    to_scalar = pltpu.make_async_copy(cnt_ref, weight_ref, count_sem)
    to_scalar.start()

    def await_e(source, chunk):
        earlier(source, chunk, col, send_e.at[source]).wait_recv()

    def hand_on(source, chunk, target):
        await_e(source, chunk)
        earlier(source, chunk, target, send_on).start()

    def both_ways(distance, chunk):
        @pl.when(col == 1)
        def _():
            hand_on(1 + distance, chunk, 0)
        @pl.when(col == n_col - 2)
        def _():
            hand_on(n_col - 2 - distance, chunk, n_col - 1)

    onward = [(d, chunk) for d in range(1, n_col - 1) for chunk in chunks]
    for distance, chunk in sorted(onward, key=lambda x: 3 * x[0] + 2 * x[1]):
        both_ways(distance, chunk)

    def arrive(n, part):
        own_out(n, part).wait_recv()
        core_out(n, part).start()

    def form(source, s):
        b = em_ref[source, 0, len(order) + s]
        wide = jnp.concatenate(
            [
                jnp.where(b == 0, lg_ref[2 * source, u], lg_ref[2 * source + 1, u])
                for u in range(slots_l)
            ],
            axis=1,
        )
        product = jnp.dot(eg_ref[source, s], wide, preferred_element_type=jnp.float32)
        for u in range(slots_l):
            p_ref[s, u] = product[:, u * side:(u + 1) * side]

    def spread(source, fresh):
        def one_row(i, carry):
            for j in range(cols):
                total = None if fresh else out_ref[i, j]
                for b in range(early_ka):
                    k = source * early_ka + b
                    s = em_ref[source, 0, b * rows + i]
                    u = lm_ref[k, 0, j]
                    term = weight_ref[i * cols + j, k] * p_ref[s, u]
                    total = term if total is None else total + term
                out_ref[i, j] = total
            return carry
        lax.fori_loop(0, rows, one_row, 0)

    def await_l(source):
        differ, _ = apart(source)
        n = lax.rem(chips - differ, chips)
        k = 2 * source + 1 - core
        for kind, ref in enumerate((lm_ref.at[k], lg_ref.at[k])):
            pltpu.make_async_copy(ref, ref, recv_core.at[n, kind]).wait()

    at_end = jnp.logical_or(col == 0, col == n_col - 1)
    last = n_col - 1 - col

    def all_columns(distant):
        def one_column(number, carry):
            source = jnp.where(col < n_col // 2, number, n_col - 1 - number)
            _, hops = apart(source)
            held_back = jnp.logical_and(at_end, source == last)
            mine = hops > 1 if distant else hops <= 1
            @pl.when(jnp.logical_and(mine, jnp.logical_not(held_back)))
            def _():
                await_l(source)
                @pl.when(jnp.logical_not(jnp.logical_or(source == col, passes(source))))
                def _():
                    for chunk in chunks:
                        await_e(source, chunk)
                for s in range(slots_e):
                    form(source, s)
                spread(source, False)
            return carry
        lax.fori_loop(0, n_col, one_column, 0)

    out_ref[...] = jnp.zeros_like(out_ref)
    for part in parts:
        for n in near:
            arrive(n, part)
    to_scalar.wait()
    all_columns(False)
    for part in parts:
        for n in far:
            arrive(n, part)
    all_columns(True)

    @pl.when(at_end)
    def _():
        await_l(last)
        for chunk in chunks:
            await_e(last, chunk)
            if chunk:
                form(last, chunk - 1)
        spread(last, False)

    drain(lm_ref.at[pl.ds(0, chips - 1)], send_own.at[0])
    drain(lg_ref.at[pl.ds(0, chips - 1)], send_own.at[1])
    drain(lm_ref.at[pl.ds(0, chips)], send_core.at[0])
    drain(lg_ref.at[pl.ds(0, chips)], send_core.at[1])
    for offset in offsets:
        target = col + offset
        @pl.when(direct_e(col, target))
        def _():
            drain(em_ref.at[col], send_e.at[target, 0])
            drain(eg_ref.at[col], send_e.at[target, 1])
    @pl.when(jnp.logical_or(col == 1, col == n_col - 2))
    def _():
        drain(em_ref.at[pl.ds(0, n_col - 2)], send_on.at[0])
        drain(eg_ref.at[pl.ds(0, n_col - 2)], send_on.at[1])


def on_device(n_row, n_col, earlier_blocks, later_blocks, earlier_pattern, later_pattern, triples):
    rows, early_ka, side, _ = earlier_blocks.shape
    late_kb, cols = later_blocks.shape[:2]
    chips = n_row // 2
    assert late_kb == 1 and early_ka == 2 and n_col >= 4
    assert n_row == 2 * chips == 2 * n_col and chips & (chips - 1) == 0
    slots_e = max(1, rows * early_ka // 2)
    slots_l = max(1, late_kb * cols // 2)
    parts = HALVES + 1
    hbm = pl.BlockSpec(memory_space=pltpu.HBM)
    block = jnp.bfloat16
    dma = pltpu.SemaphoreType.DMA
    return pl.pallas_call(
        functools.partial(kernel, n_row, n_col),
        out_shape=jax.ShapeDtypeStruct((rows, cols, side, side), jnp.float32),
        in_specs=[hbm] * 5,
        out_specs=pl.BlockSpec(memory_space=pltpu.VMEM),
        scratch_shapes=[
            pltpu.VMEM(earlier_blocks.shape, block),
            pltpu.VMEM(later_blocks.shape, block),
            pltpu.VMEM(triples.shape, jnp.int32),
            pltpu.SMEM((early_ka, rows), jnp.int32),
            pltpu.SMEM(later_pattern.shape, jnp.int32),
            pltpu.VMEM((n_col, slots_e, side, side), block),
            pltpu.VMEM((n_row, slots_l, side, side), block),
            pltpu.SMEM((n_col, 1, LANES), jnp.int32),
            pltpu.SMEM((n_row, 1, LANES), jnp.int32),
            pltpu.VMEM((rows * cols, LANES), jnp.float32),
            pltpu.SMEM((rows * cols, LANES), jnp.float32),
            pltpu.VMEM((slots_e + 1, slots_l + 1, side, side), jnp.float32),
            dma((5,)),
            dma(()),
            pltpu.SemaphoreType.REGULAR,
            dma((n_col, 2)),
            dma((n_col, slots_e + 1)),
            dma((2,)),
            dma((2,)),
            dma((chips - 1, parts)),
            dma((2,)),
            dma((chips, 2)),
        ],
        compiler_params=pltpu.CompilerParams(
            collective_id=0, has_side_effects=True, vmem_limit_bytes=32 << 20
        ),
        name="gather_compose",
    )(*(
        pltpu.with_memory_space_constraint(x, pltpu.HBM)
        for x in (earlier_blocks, later_blocks, earlier_pattern.T, later_pattern, triples)
    ))


def solution(mesh):
    return jax.shard_map(
        functools.partial(on_device, mesh.shape["row"], mesh.shape["col"]),
        mesh=mesh,
        in_specs=(
            P("row", "col", None, None),
            P("row", "col", None, None),
            P("row", "col"),
            P("row", "col"),
            P("row", "col", None),
        ),
        out_specs=P("row", "col", None, None),
        check_vma=False,
    )
```

```python
import functools

import jax
import jax.numpy as jnp
from jax import lax
from jax.experimental import pallas as pl
from jax.experimental.pallas import tpu as pltpu
from jax.sharding import PartitionSpec as P

MESH = pl.DeviceIdType.MESH
LANES = 128
HALVES = 2


def ranks(live):
    out, rank = [], jnp.int32(0)
    for flag in live:
        out.append(rank)
        rank = rank + flag
    return out


def entry_of_slot(live, rank, slot):
    entry = jnp.int32(0)
    for number, (flag, place) in enumerate(zip(live, rank)):
        entry = entry + jnp.where(jnp.logical_and(flag == 1, place == slot), number, 0)
    return entry


def kernel(
    n_row, n_col,
    e_hbm, l_hbm, ep_hbm, lp_hbm, t_hbm,
    out_ref,
    e_ref, l_ref, t_ref, ep_ref, lp_ref,
    eg_ref, lg_ref, em_ref, lm_ref, cnt_ref, weight_ref, p_ref,
    fetch_sem, count_sem, ready_sem,
    send_e, recv_e, send_on, send_own, recv_own, send_core, recv_core,
):
    rows, early_ka, side, _ = e_ref.shape
    cols = l_ref.shape[1]
    slots_e, slots_l = eg_ref.shape[1], lg_ref.shape[1]
    row, col = lax.axis_index("row"), lax.axis_index("col")
    core, chip = lax.rem(row, 2), row // 2
    chips = n_row // 2
    bits = range(chips.bit_length() - 1)

    fetches = [
        pltpu.make_async_copy(src, dst, fetch_sem.at[n])
        for n, (src, dst) in enumerate((
            (ep_hbm, ep_ref), (lp_hbm, lp_ref), (e_hbm, e_ref), (l_hbm, l_ref), (t_hbm, t_ref),
        ))
    ]
    for copy in fetches:
        copy.start()

    def digits(number):
        return [lax.rem(number // 2**b, 2) for b in bits]

    def moved(m):
        return sum((1 - v if m >> b & 1 else v) * 2**b for b, v in zip(bits, digits(chip)))

    def apart(there):
        differ = [v + w - 2 * v * w for v, w in zip(digits(chip), digits(there))]
        return sum(v * 2**b for b, v in zip(bits, differ)), sum(differ)

    chip_of = [chip] + [moved(chips - n) for n in range(1, chips)]
    near = [n for n in range(chips - 1, 0, -1) if (chips - n).bit_count() == 1]
    far = [n for n in range(1, chips) if n not in near]
    vouched = chips == 4
    partner = (row + 1 - 2 * core, col)

    def place(n):
        return (2 * chip_of[n] + core, col)

    def on_line(number):
        return jnp.logical_and(number >= 0, number < n_col)

    toward = jnp.where(col < n_col // 2, 1, -1)
    at_end = jnp.logical_or(col == 0, col == n_col - 1)

    barrier = pltpu.get_barrier_semaphore()
    greeted = [place(n) for n in (near if vouched else near + far)] + [partner]
    expected = jnp.int32(len(greeted))
    for step in (1, -1):
        @pl.when(on_line(col + step))
        def _():
            pl.semaphore_signal(
                barrier, inc=1, device_id=(row, col + step), device_id_type=MESH
            )
        expected = expected + on_line(col + step).astype(jnp.int32)
    for device in greeted:
        pl.semaphore_signal(barrier, inc=1, device_id=device, device_id_type=MESH)

    def remote(src, dst, send, recv, device):
        return pltpu.make_async_remote_copy(
            src_ref=src, dst_ref=dst, send_sem=send, recv_sem=recv,
            device_id=device, device_id_type=MESH,
        )

    chunks = range(slots_e + 1)

    def earlier(source, chunk, target, send):
        ref = em_ref.at[source] if chunk == 0 else eg_ref.at[source, chunk - 1]
        return remote(
            ref, ref, send.at[min(chunk, 1)], recv_e.at[source, chunk], (row, target)
        )

    half = slots_l // HALVES
    parts = range(HALVES + 1)

    def later_ref(source, part):
        if part == 0:
            return lm_ref.at[source]
        return lg_ref.at[source, pl.ds((part - 1) * half, half)]

    def own_out(n, part):
        ref = later_ref(row, part)
        return remote(ref, ref, send_own.at[min(part, 1)], recv_own.at[n - 1, part], place(n))

    def core_out(n, part):
        ref = later_ref(2 * chip_of[n] + core, part)
        kind = min(part, 1)
        return remote(ref, ref, send_core.at[kind], recv_core.at[n, kind], partner)

    def drain(ref, sem):
        pltpu.make_async_copy(ref, ref, sem).wait()

    order = [(a, b) for b in range(early_ka) for a in range(rows)]
    fetches[0].wait()
    live = [ep_ref[b, a] for a, b in order]
    rank = ranks(live)
    picks_e = [entry_of_slot(live, rank, s) for s in range(slots_e)]
    for n, (flag, spot) in enumerate(zip(live, rank)):
        em_ref[col, 0, n] = jnp.where(flag == 1, spot, slots_e)
    for s, entry in enumerate(picks_e):
        em_ref[col, 0, len(order) + s] = entry // rows
    fetches[2].wait()
    for s, entry in enumerate(picks_e):
        eg_ref[col, s] = e_ref[lax.rem(entry, rows), entry // rows]
    pl.semaphore_wait(barrier, expected)
    if vouched:
        pl.semaphore_signal(ready_sem, inc=1, device_id=place(near[0]), device_id_type=MESH)
    for n, step in enumerate((-1, 1)):
        @pl.when(on_line(col + step))
        def _():
            for chunk in chunks:
                earlier(col, chunk, col + step, send_e.at[n]).start()

    fetches[1].wait()
    live = [lp_ref[0, j] for j in range(cols)]
    rank = ranks(live)
    picks_l = [entry_of_slot(live, rank, s) for s in range(slots_l)]
    for n, (flag, spot) in enumerate(zip(live, rank)):
        lm_ref[row, 0, n] = jnp.where(flag == 1, spot, slots_l)
    fetches[3].wait()
    for s, entry in enumerate(picks_l):
        lg_ref[row, s] = l_ref[0, entry]
    for n in near:
        for part in parts:
            own_out(n, part).start()
    for part in parts:
        core_out(0, part).start()
    for s in range(slots_e + 1):
        p_ref[s, slots_l] = jnp.zeros((side, side), jnp.float32)
    for u in range(slots_l):
        p_ref[slots_e, u] = jnp.zeros((side, side), jnp.float32)
    fetches[4].wait()
    middle = n_row
    lane = lax.broadcasted_iota(jnp.int32, (cols, LANES), 1)
    for i in range(rows):
        numbers = t_ref[i]
        counts = jnp.zeros((cols, LANES), jnp.float32)
        for k in range(middle):
            hits = jnp.sum(jnp.where(numbers == k, 1.0, 0.0), axis=1, keepdims=True)
            counts = jnp.where(lane == k, hits, counts)
        cnt_ref[i * cols:(i + 1) * cols, :] = counts
    to_scalar = pltpu.make_async_copy(cnt_ref, weight_ref, count_sem)
    to_scalar.start()

    def await_e(source, chunk):
        earlier(source, chunk, col, send_on).wait_recv()

    def hand_on(distance, turn):
        sign = toward if turn == 0 else -toward
        source = col + sign * distance
        @pl.when(jnp.logical_and(on_line(source), on_line(col - sign)))
        def _():
            for chunk in chunks:
                await_e(source, chunk)
                earlier(source, chunk, col - sign, send_on).start()

    for distance in range(1, n_col - 1):
        for turn in range(2):
            hand_on(distance, turn)
            if distance == 1 and turn == 0:
                if vouched:
                    pl.semaphore_wait(ready_sem, 1)
                for n in far:
                    for part in parts:
                        own_out(n, part).start()

    def arrive(n, part):
        own_out(n, part).wait_recv()
        core_out(n, part).start()

    def form(source, s):
        b = em_ref[source, 0, len(order) + s]
        wide = jnp.concatenate(
            [
                jnp.where(b == 0, lg_ref[2 * source, u], lg_ref[2 * source + 1, u])
                for u in range(slots_l)
            ],
            axis=1,
        )
        product = jnp.dot(eg_ref[source, s], wide, preferred_element_type=jnp.float32)
        for u in range(slots_l):
            p_ref[s, u] = product[:, u * side:(u + 1) * side]

    def spread(source, fresh):
        def one_row(i, carry):
            for j in range(cols):
                total = None if fresh else out_ref[i, j]
                for b in range(early_ka):
                    k = source * early_ka + b
                    s = em_ref[source, 0, b * rows + i]
                    u = lm_ref[k, 0, j]
                    term = weight_ref[i * cols + j, k] * p_ref[s, u]
                    total = term if total is None else total + term
                out_ref[i, j] = total
            return carry
        lax.fori_loop(0, rows, one_row, 0)

    def await_l(source):
        differ, _ = apart(source)
        n = lax.rem(chips - differ, chips)
        k = 2 * source + 1 - core
        for kind, ref in enumerate((lm_ref.at[k], lg_ref.at[k])):
            pltpu.make_async_copy(ref, ref, recv_core.at[n, kind]).wait()

    last = n_col - 1 - col

    def all_columns(distant):
        def one_column(number, carry):
            source = jnp.where(col < n_col // 2, number, n_col - 1 - number)
            _, hops = apart(source)
            held_back = jnp.logical_and(at_end, source == last)
            soon = jnp.logical_and(hops <= 1, number < 2)
            mine = jnp.logical_not(soon) if distant else soon
            @pl.when(jnp.logical_and(mine, jnp.logical_not(held_back)))
            def _():
                await_l(source)
                @pl.when(jnp.logical_and(source != col, at_end))
                def _():
                    for chunk in chunks:
                        await_e(source, chunk)
                for s in range(slots_e):
                    form(source, s)
                spread(source, False)
            return carry
        lax.fori_loop(0, n_col, one_column, 0)

    out_ref[...] = jnp.zeros_like(out_ref)
    for part in parts:
        for n in near:
            arrive(n, part)
    to_scalar.wait()
    all_columns(False)
    for part in parts:
        for n in far:
            arrive(n, part)
    all_columns(True)

    @pl.when(at_end)
    def _():
        await_l(last)
        for chunk in chunks:
            await_e(last, chunk)
            if chunk:
                form(last, chunk - 1)
        spread(last, False)

    drain(lm_ref.at[pl.ds(0, chips - 1)], send_own.at[0])
    drain(lg_ref.at[pl.ds(0, chips - 1)], send_own.at[1])
    drain(lm_ref.at[pl.ds(0, chips)], send_core.at[0])
    drain(lg_ref.at[pl.ds(0, chips)], send_core.at[1])
    for n, step in enumerate((-1, 1)):
        @pl.when(on_line(col + step))
        def _():
            drain(em_ref.at[col], send_e.at[n, 0])
            drain(eg_ref.at[col], send_e.at[n, 1])
    @pl.when(jnp.logical_not(at_end))
    def _():
        drain(em_ref.at[pl.ds(0, n_col - 1)], send_on.at[0])
        drain(eg_ref.at[pl.ds(0, n_col - 1)], send_on.at[1])


def on_device(n_row, n_col, earlier_blocks, later_blocks, earlier_pattern, later_pattern, triples):
    rows, early_ka, side, _ = earlier_blocks.shape
    late_kb, cols = later_blocks.shape[:2]
    chips = n_row // 2
    assert late_kb == 1 and early_ka == 2 and n_col >= 4
    assert n_row == 2 * chips == 2 * n_col and chips & (chips - 1) == 0
    slots_e = max(1, rows * early_ka // 2)
    slots_l = max(1, late_kb * cols // 2)
    parts = HALVES + 1
    hbm = pl.BlockSpec(memory_space=pltpu.HBM)
    block = jnp.bfloat16
    dma = pltpu.SemaphoreType.DMA
    return pl.pallas_call(
        functools.partial(kernel, n_row, n_col),
        out_shape=jax.ShapeDtypeStruct((rows, cols, side, side), jnp.float32),
        in_specs=[hbm] * 5,
        out_specs=pl.BlockSpec(memory_space=pltpu.VMEM),
        scratch_shapes=[
            pltpu.VMEM(earlier_blocks.shape, block),
            pltpu.VMEM(later_blocks.shape, block),
            pltpu.VMEM(triples.shape, jnp.int32),
            pltpu.SMEM((early_ka, rows), jnp.int32),
            pltpu.SMEM(later_pattern.shape, jnp.int32),
            pltpu.VMEM((n_col, slots_e, side, side), block),
            pltpu.VMEM((n_row, slots_l, side, side), block),
            pltpu.SMEM((n_col, 1, LANES), jnp.int32),
            pltpu.SMEM((n_row, 1, LANES), jnp.int32),
            pltpu.VMEM((rows * cols, LANES), jnp.float32),
            pltpu.SMEM((rows * cols, LANES), jnp.float32),
            pltpu.VMEM((slots_e + 1, slots_l + 1, side, side), jnp.float32),
            dma((5,)),
            dma(()),
            pltpu.SemaphoreType.REGULAR,
            dma((2, 2)),
            dma((n_col, slots_e + 1)),
            dma((2,)),
            dma((2,)),
            dma((chips - 1, parts)),
            dma((2,)),
            dma((chips, 2)),
        ],
        compiler_params=pltpu.CompilerParams(
            collective_id=0, has_side_effects=True, vmem_limit_bytes=32 << 20
        ),
        name="gather_compose",
    )(*(
        pltpu.with_memory_space_constraint(x, pltpu.HBM)
        for x in (earlier_blocks, later_blocks, earlier_pattern.T, later_pattern, triples)
    ))


def solution(mesh):
    return jax.shard_map(
        functools.partial(on_device, mesh.shape["row"], mesh.shape["col"]),
        mesh=mesh,
        in_specs=(
            P("row", "col", None, None),
            P("row", "col", None, None),
            P("row", "col"),
            P("row", "col"),
            P("row", "col", None),
        ),
        out_specs=P("row", "col", None, None),
        check_vma=False,
    )
```

```python
import functools

import jax
import jax.numpy as jnp
from jax import lax
from jax.experimental import pallas as pl
from jax.experimental.pallas import tpu as pltpu
from jax.sharding import PartitionSpec as P

MESH = pl.DeviceIdType.MESH
LANES = 128
HALVES = 2


def ranks(live):
    out, rank = [], jnp.int32(0)
    for flag in live:
        out.append(rank)
        rank = rank + flag
    return out


def entry_of_slot(live, rank, slot):
    entry = jnp.int32(0)
    for number, (flag, place) in enumerate(zip(live, rank)):
        entry = entry + jnp.where(jnp.logical_and(flag == 1, place == slot), number, 0)
    return entry


def kernel(
    n_row, n_col,
    e_hbm, l_hbm, ep_hbm, lp_hbm, t_hbm,
    out_ref,
    e_ref, l_ref, t_ref, ep_ref, lp_ref,
    eg_ref, lg_ref, em_ref, lm_ref, cnt_ref, weight_ref, p_ref,
    fetch_sem, count_sem, ready_sem,
    send_e, recv_e, send_on, send_own, recv_own, send_core, recv_core,
):
    rows, early_ka, side, _ = e_ref.shape
    cols = l_ref.shape[1]
    slots_e, slots_l = eg_ref.shape[1], lg_ref.shape[1]
    row, col = lax.axis_index("row"), lax.axis_index("col")
    core, chip = lax.rem(row, 2), row // 2
    chips = n_row // 2
    bits = range(chips.bit_length() - 1)

    fetches = [
        pltpu.make_async_copy(src, dst, fetch_sem.at[n])
        for n, (src, dst) in enumerate((
            (ep_hbm, ep_ref), (lp_hbm, lp_ref), (e_hbm, e_ref), (l_hbm, l_ref), (t_hbm, t_ref),
        ))
    ]
    for copy in fetches:
        copy.start()

    def digits(number):
        return [lax.rem(number // 2**b, 2) for b in bits]

    def moved(m):
        return sum((1 - v if m >> b & 1 else v) * 2**b for b, v in zip(bits, digits(chip)))

    def apart(there):
        differ = [v + w - 2 * v * w for v, w in zip(digits(chip), digits(there))]
        return sum(v * 2**b for b, v in zip(bits, differ)), sum(differ)

    chip_of = [chip] + [moved(chips - n) for n in range(1, chips)]
    near = [n for n in range(chips - 1, 0, -1) if (chips - n).bit_count() == 1]
    far = [n for n in range(1, chips) if n not in near]
    vouched = chips == 4
    partner = (row + 1 - 2 * core, col)

    def place(n):
        return (2 * chip_of[n] + core, col)

    def on_line(number):
        return jnp.logical_and(number >= 0, number < n_col)

    toward = jnp.where(col < n_col // 2, 1, -1)
    at_end = jnp.logical_or(col == 0, col == n_col - 1)
    skips = n_col == 4
    leaper = jnp.logical_and(core == 0, col == n_col - 1)
    skipped = jnp.logical_and(core == 0, col == n_col - 2)
    landing = jnp.logical_and(core == 0, col == n_col - 3)

    barrier = pltpu.get_barrier_semaphore()
    greeted = [place(n) for n in (near if vouched else near + far)] + [partner]
    expected = jnp.int32(len(greeted))
    for step in (1, -1):
        @pl.when(on_line(col + step))
        def _():
            pl.semaphore_signal(
                barrier, inc=1, device_id=(row, col + step), device_id_type=MESH
            )
        expected = expected + on_line(col + step).astype(jnp.int32)
    if skips:
        @pl.when(landing)
        def _():
            pl.semaphore_signal(
                barrier, inc=1, device_id=(row, col + 2), device_id_type=MESH
            )
        expected = expected + leaper.astype(jnp.int32)
    for device in greeted:
        pl.semaphore_signal(barrier, inc=1, device_id=device, device_id_type=MESH)

    def remote(src, dst, send, recv, device):
        return pltpu.make_async_remote_copy(
            src_ref=src, dst_ref=dst, send_sem=send, recv_sem=recv,
            device_id=device, device_id_type=MESH,
        )

    chunks = range(slots_e + 1)

    def earlier(source, chunk, target, send):
        ref = em_ref.at[source] if chunk == 0 else eg_ref.at[source, chunk - 1]
        return remote(
            ref, ref, send.at[min(chunk, 1)], recv_e.at[source, chunk], (row, target)
        )

    half = slots_l // HALVES
    parts = range(HALVES + 1)

    def later_ref(source, part):
        if part == 0:
            return lm_ref.at[source]
        return lg_ref.at[source, pl.ds((part - 1) * half, half)]

    def own_out(n, part):
        ref = later_ref(row, part)
        return remote(ref, ref, send_own.at[min(part, 1)], recv_own.at[n - 1, part], place(n))

    def core_out(n, part):
        ref = later_ref(2 * chip_of[n] + core, part)
        kind = min(part, 1)
        return remote(ref, ref, send_core.at[kind], recv_core.at[n, kind], partner)

    def drain(ref, sem):
        pltpu.make_async_copy(ref, ref, sem).wait()

    order = [(a, b) for b in range(early_ka) for a in range(rows)]
    fetches[0].wait()
    live = [ep_ref[b, a] for a, b in order]
    rank = ranks(live)
    picks_e = [entry_of_slot(live, rank, s) for s in range(slots_e)]
    for n, (flag, spot) in enumerate(zip(live, rank)):
        em_ref[col, 0, n] = jnp.where(flag == 1, spot, slots_e)
    for s, entry in enumerate(picks_e):
        em_ref[col, 0, len(order) + s] = entry // rows
    fetches[2].wait()
    for s, entry in enumerate(picks_e):
        eg_ref[col, s] = e_ref[lax.rem(entry, rows), entry // rows]
    pl.semaphore_wait(barrier, expected)
    if vouched:
        pl.semaphore_signal(ready_sem, inc=1, device_id=place(near[0]), device_id_type=MESH)
    if skips:
        @pl.when(leaper)
        def _():
            for chunk in chunks:
                earlier(col, chunk, col - 2, send_e.at[1]).start()
    for n, step in enumerate((-1, 1)):
        @pl.when(on_line(col + step))
        def _():
            for chunk in chunks:
                earlier(col, chunk, col + step, send_e.at[n]).start()

    fetches[1].wait()
    live = [lp_ref[0, j] for j in range(cols)]
    rank = ranks(live)
    picks_l = [entry_of_slot(live, rank, s) for s in range(slots_l)]
    for n, (flag, spot) in enumerate(zip(live, rank)):
        lm_ref[row, 0, n] = jnp.where(flag == 1, spot, slots_l)
    fetches[3].wait()
    for s, entry in enumerate(picks_l):
        lg_ref[row, s] = l_ref[0, entry]
    for n in near:
        for part in parts:
            own_out(n, part).start()
    for part in parts:
        core_out(0, part).start()
    out_ref[...] = jnp.zeros_like(out_ref)
    for at in range(2):
        for s in range(slots_e + 1):
            p_ref[at, s, slots_l] = jnp.zeros((side, side), jnp.float32)
        for u in range(slots_l):
            p_ref[at, slots_e, u] = jnp.zeros((side, side), jnp.float32)
    fetches[4].wait()
    middle = n_row
    lane = lax.broadcasted_iota(jnp.int32, (cols, LANES), 1)
    for i in range(rows):
        numbers = t_ref[i]
        counts = jnp.zeros((cols, LANES), jnp.float32)
        for k in range(middle):
            hits = jnp.sum(jnp.where(numbers == k, 1.0, 0.0), axis=1, keepdims=True)
            counts = jnp.where(lane == k, hits, counts)
        cnt_ref[i * cols:(i + 1) * cols, :] = counts
    to_scalar = pltpu.make_async_copy(cnt_ref, weight_ref, count_sem)
    to_scalar.start()

    def arrive(n, part):
        own_out(n, part).wait_recv()
        core_out(n, part).start()

    def await_e(source, chunk):
        earlier(source, chunk, col, send_on).wait_recv()

    def hand_on(distance, turn):
        sign = toward if turn == 0 else -toward
        source = col + sign * distance
        wanted = jnp.logical_and(on_line(source), on_line(col - sign))
        if skips:
            wanted = jnp.logical_and(wanted, jnp.logical_not(landing))
        @pl.when(wanted)
        def _():
            for chunk in chunks:
                await_e(source, chunk)
                if skips and turn == 1 and distance == 1:
                    @pl.when(jnp.logical_not(skipped))
                    def _():
                        earlier(source, chunk, col - sign, send_on).start()
                else:
                    earlier(source, chunk, col - sign, send_on).start()

    if vouched:
        pl.semaphore_wait(ready_sem, 1)
    for n in far:
        for part in parts:
            own_out(n, part).start()

    if skips:
        @pl.when(landing)
        def _():
            both = [(d, chunk) for d in (1, 2) for chunk in chunks]
            for at, (d, chunk) in enumerate(sorted(both, key=lambda x: 3 * x[0] + 2 * x[1])):
                await_e(col + d, chunk)
                earlier(col + d, chunk, col - 1, send_on).start()
                if at == 1:
                    for other in chunks:
                        await_e(col - 1, other)
                        earlier(col - 1, other, col + 1, send_on).start()

    for distance in range(1, n_col - 1):
        for turn in range(2):
            hand_on(distance, turn)
        if distance == 1:
            for part in parts:
                for n in near:
                    arrive(n, part)

    def form(source, s, at=0):
        b = em_ref[source, 0, len(order) + s]
        wide = jnp.concatenate(
            [
                jnp.where(b == 0, lg_ref[2 * source, u], lg_ref[2 * source + 1, u])
                for u in range(slots_l)
            ],
            axis=1,
        )
        product = jnp.dot(eg_ref[source, s], wide, preferred_element_type=jnp.float32)
        for u in range(slots_l):
            p_ref[at, s, u] = product[:, u * side:(u + 1) * side]

    def spread(source, at=0):
        def one_row(i, carry):
            for j in range(cols):
                total = out_ref[i, j]
                for b in range(early_ka):
                    k = source * early_ka + b
                    s = em_ref[source, 0, b * rows + i]
                    u = lm_ref[k, 0, j]
                    total = total + weight_ref[i * cols + j, k] * p_ref[at, s, u]
                out_ref[i, j] = total
            return carry
        lax.fori_loop(0, rows, one_row, 0)

    def await_l(source):
        differ, _ = apart(source)
        n = lax.rem(chips - differ, chips)
        k = 2 * source + 1 - core
        for kind, ref in enumerate((lm_ref.at[k], lg_ref.at[k])):
            pltpu.make_async_copy(ref, ref, recv_core.at[n, kind]).wait()

    last = n_col - 1 - col
    second = last - toward

    def all_columns(distant):
        def one_column(number, carry):
            late = number >= n_col
            number = lax.rem(number, n_col)
            source = jnp.where(col < n_col // 2, number, n_col - 1 - number)
            _, hops = apart(source)
            held_back = jnp.logical_and(
                at_end, jnp.logical_or(source == last, source == second)
            )
            soon = jnp.logical_and(at_end, jnp.logical_and(hops <= 1, number < 2))
            mine = soon
            if distant:
                mine = jnp.logical_and(jnp.logical_not(soon), late == (hops > 1))
            @pl.when(jnp.logical_and(mine, jnp.logical_not(held_back)))
            def _():
                await_l(source)
                @pl.when(jnp.logical_and(source != col, at_end))
                def _():
                    for chunk in chunks:
                        await_e(source, chunk)
                for s in range(slots_e):
                    form(source, s)
                spread(source)
            return carry
        lax.fori_loop(0, 2 * n_col if distant else n_col, one_column, 0)

    to_scalar.wait()
    all_columns(False)
    for part in parts:
        for n in far:
            arrive(n, part)
    all_columns(True)

    @pl.when(at_end)
    def _():
        await_l(second)
        await_l(last)
        both = [(at, chunk) for at in range(2) for chunk in chunks]
        for at, chunk in sorted(both, key=lambda x: 3 * x[0] + 2 * x[1]):
            source = (second, last)[at]
            await_e(source, chunk)
            if chunk:
                form(source, chunk - 1, at)
            if chunk == slots_e:
                spread(source, at)

    drain(lm_ref.at[pl.ds(0, chips - 1)], send_own.at[0])
    drain(lg_ref.at[pl.ds(0, chips - 1)], send_own.at[1])
    drain(lm_ref.at[pl.ds(0, chips)], send_core.at[0])
    drain(lg_ref.at[pl.ds(0, chips)], send_core.at[1])
    for n, step in enumerate((-1, 1)):
        @pl.when(on_line(col + step))
        def _():
            drain(em_ref.at[col], send_e.at[n, 0])
            drain(eg_ref.at[col], send_e.at[n, 1])
    if skips:
        @pl.when(leaper)
        def _():
            drain(em_ref.at[col], send_e.at[1, 0])
            drain(eg_ref.at[col], send_e.at[1, 1])
        @pl.when(skipped)
        def _():
            drain(em_ref.at[pl.ds(0, n_col - 2)], send_on.at[0])
            drain(eg_ref.at[pl.ds(0, n_col - 2)], send_on.at[1])
    full = jnp.logical_not(at_end)
    if skips:
        full = jnp.logical_and(full, jnp.logical_not(skipped))
    @pl.when(full)
    def _():
        drain(em_ref.at[pl.ds(0, n_col - 1)], send_on.at[0])
        drain(eg_ref.at[pl.ds(0, n_col - 1)], send_on.at[1])


def on_device(n_row, n_col, earlier_blocks, later_blocks, earlier_pattern, later_pattern, triples):
    rows, early_ka, side, _ = earlier_blocks.shape
    late_kb, cols = later_blocks.shape[:2]
    chips = n_row // 2
    assert late_kb == 1 and early_ka == 2 and n_col >= 4
    assert n_row == 2 * chips == 2 * n_col and chips & (chips - 1) == 0
    slots_e = max(1, rows * early_ka // 2)
    slots_l = max(1, late_kb * cols // 2)
    parts = HALVES + 1
    hbm = pl.BlockSpec(memory_space=pltpu.HBM)
    block = jnp.bfloat16
    dma = pltpu.SemaphoreType.DMA
    return pl.pallas_call(
        functools.partial(kernel, n_row, n_col),
        out_shape=jax.ShapeDtypeStruct((rows, cols, side, side), jnp.float32),
        in_specs=[hbm] * 5,
        out_specs=pl.BlockSpec(memory_space=pltpu.VMEM),
        scratch_shapes=[
            pltpu.VMEM(earlier_blocks.shape, block),
            pltpu.VMEM(later_blocks.shape, block),
            pltpu.VMEM(triples.shape, jnp.int32),
            pltpu.SMEM((early_ka, rows), jnp.int32),
            pltpu.SMEM(later_pattern.shape, jnp.int32),
            pltpu.VMEM((n_col, slots_e, side, side), block),
            pltpu.VMEM((n_row, slots_l, side, side), block),
            pltpu.SMEM((n_col, 1, LANES), jnp.int32),
            pltpu.SMEM((n_row, 1, LANES), jnp.int32),
            pltpu.VMEM((rows * cols, LANES), jnp.float32),
            pltpu.SMEM((rows * cols, LANES), jnp.float32),
            pltpu.VMEM((2, slots_e + 1, slots_l + 1, side, side), jnp.float32),
            dma((5,)),
            dma(()),
            pltpu.SemaphoreType.REGULAR,
            dma((2, 2)),
            dma((n_col, slots_e + 1)),
            dma((2,)),
            dma((2,)),
            dma((chips - 1, parts)),
            dma((2,)),
            dma((chips, 2)),
        ],
        compiler_params=pltpu.CompilerParams(
            collective_id=0, has_side_effects=True, vmem_limit_bytes=32 << 20
        ),
        name="gather_compose",
    )(*(
        pltpu.with_memory_space_constraint(x, pltpu.HBM)
        for x in (earlier_blocks, later_blocks, earlier_pattern.T, later_pattern, triples)
    ))


def solution(mesh):
    return jax.shard_map(
        functools.partial(on_device, mesh.shape["row"], mesh.shape["col"]),
        mesh=mesh,
        in_specs=(
            P("row", "col", None, None),
            P("row", "col", None, None),
            P("row", "col"),
            P("row", "col"),
            P("row", "col", None),
        ),
        out_specs=P("row", "col", None, None),
        check_vma=False,
    )
```
